768 devices in a mesh: wave: 48 (over y, z_hi, core), atom: 16 (over x, z_lo).
Axes of the slice: x: 4, y: 8, z: 12 (z_hi: 3, z_lo: 4; z = z_hi * 4 + z_lo), core: 2. Of those that a mesh axis runs over, the one named last changes fastest.
Arguments:
- slab: float32 [24576, 2048], P('wave', 'atom'), may hold values from -0.0390625 to 0.0390625
- orbitals: float32 [24576, 256], P('wave'), may hold values from -6 to 6
- sphere_ops: float32 [3, 32, 64, 64], P(None, 'atom'), may hold values from -0.75 to 0.75
- wave_terms: float32 [3, 24576], P(None, 'wave'), may hold values from -1 to 1
Outputs:
- applied: float32 [3, 24576, 256], P(None, ('wave', 'atom'))
The draws below stay inside these ranges and needn't reach their ends.
All inputs are finite; a program needn't handle non-finite values.
Results may differ from the reference program's by a relative error of at most 0.0001.
Values sent between devices are 32-bit elements; how exact they have to be, the bound alone decides.
No kernel may reach another device: no remote copies, remote signals or barrier semaphores. Data moves between devices by JAX's collectives and lax.ppermute only.
A program may use at most 32 MiB of HBM per device.

```python
import jax
import jax.numpy as jnp
from jax import lax

LM = 64
NB = 256
NW = 24576
ATOMS = 32
NS = 2048


def shard_levels(own_key, extent, cuts, low, high):
    def one(axis_at, parts):
        steps = jax.random.uniform(jax.random.fold_in(jax.random.fold_in(own_key, 6), axis_at), (parts,), jnp.float32, low / len(cuts), high / len(cuts))
        return jnp.repeat(jnp.exp(steps), extent[axis_at] // parts).reshape((-1,) + (1,) * (len(extent) - axis_at - 1))

    factor_of = one(*cuts[0])
    for cut in cuts[1:]:
        factor_of = factor_of * one(*cut)
    return factor_of


def normal_values(stream_key, extent, deviation, reach, pieces=(), kind=jnp.bfloat16):
    entries = jax.random.normal(stream_key, extent, jnp.float32) * deviation
    if len(pieces) > 0:
        entries = shard_levels(stream_key, extent, pieces, -0.22, 0.18) * entries
    return jnp.clip(entries, min=-reach, max=reach).astype(kind)


def setup_inputs(seed: int = 0) -> dict:
    key_of = jax.random.split(jax.random.key(seed), 5)
    slab = normal_values(key_of[0], (NW, NS), NW ** -0.5, 0.0390625, ((0, 48), (1, 16)), jnp.float32)
    orbitals = normal_values(key_of[1], (NW, NB), 1.0, 6.0, ((0, 48),), jnp.float32)
    sphere_ops = normal_values(key_of[2], (3, ATOMS, LM, LM), LM ** -0.5, 0.75, ((1, 16),), jnp.float32)
    wave_terms = jnp.clip(jax.random.uniform(key_of[3], (3, NW), jnp.float32, -1.0, 1.0) * shard_levels(key_of[3], (3, NW), ((1, 48),), -0.4, 0.0), -1.0, 1.0)
    return dict(slab=slab, orbitals=orbitals, sphere_ops=sphere_ops, wave_terms=wave_terms)


def reference(slab, orbitals, sphere_ops, wave_terms):
    coeffs = jnp.dot(slab.T, orbitals, preferred_element_type=jnp.float32, precision=lax.Precision.HIGHEST)
    blocks = coeffs.reshape(ATOMS, LM, NB)
    outs = []
    for direction in range(3):
        inner = jnp.einsum("alm,amb->alb", sphere_ops[direction], blocks, precision=lax.Precision.HIGHEST).reshape(NS, NB)
        sphere_part = jnp.dot(slab, inner, preferred_element_type=jnp.float32, precision=lax.Precision.HIGHEST)
        outs.append(sphere_part + wave_terms[direction][:, None] * orbitals)
    return jnp.stack(outs, 0)
```

```python
import jax
import jax.numpy as jnp
from jax import lax
from jax.experimental import pallas as pl
from jax.experimental.pallas import tpu as pltpu
from jax.sharding import Mesh, PartitionSpec as P


GATHER, REDUCE = "zl", "x"
THIRD, FOURTH = ("zh",), ("y", GATHER)
VMEM = pl.BlockSpec(memory_space=pltpu.VMEM)


def exchange(blocks, axes):
    return lax.all_to_all(blocks, axes, 0, 0, tiled=True)


def gather(block, axes):
    n = lax.axis_size(axes)
    return exchange(jnp.broadcast_to(block[None], (n,) + block.shape), axes)


def swap(block, axis, bit):
    n = lax.axis_size(axis)
    return lax.ppermute(block, axis, [(i, i ^ bit) for i in range(n)])


def split(a):
    high = a.astype(jnp.bfloat16)
    return high, (a - high.astype(jnp.float32)).astype(jnp.bfloat16)


def dot3(a, b, dims=(((1,), (0,)), ((), ()))):
    (ah, al), (bh, bl) = a, b
    f = lambda u, v: lax.dot_general(u, v, dims, preferred_element_type=jnp.float32)
    return f(ah, bh) + (f(ah, bl) + f(al, bh))


def first_kernel(slab_ref, orb_ref, out_ref):
    n, sub, half = out_ref.shape
    nc = orb_ref.shape[1] // half
    part = dot3(split(slab_ref[...].T), split(orb_ref[...]))
    for y in range(n // nc):
        for c in range(nc):
            out_ref[y * nc + c] = part[y * sub : (y + 1) * sub, c * half : (c + 1) * half]


def apply(slab, orbitals, sphere_ops, wave_terms):
    ny, nzh, nc, nx, nzl = (lax.axis_size(n) for n in ("y", "zh", "c", "x", "zl"))
    ng, nr = lax.axis_size(GATHER), lax.axis_size(REDUCE)
    rows, width = slab.shape
    nb = orbitals.shape[1]
    half = nb // nc
    own_rows = rows // (nx * nzl)
    nd, atoms, lm = sphere_ops.shape[:3]
    sub = width // ny
    me, core = lax.axis_index(GATHER), lax.axis_index("c")
    f32 = lambda *s: jax.ShapeDtypeStruct(s, jnp.float32)

    part = pl.pallas_call(
        first_kernel, out_shape=f32(ny * nc, sub, half), in_specs=[VMEM] * 2, out_specs=VMEM, name="first_dot"
    )(slab, orbitals)
    mine = exchange(part, ("y", "c"))

    n_slab, n_ops = nr * own_rows, nd * lm // nc
    rowset = slab.reshape(nx, nzl, own_rows, width)
    pick = lambda j: lax.dynamic_index_in_dim(
        rowset, jnp.bitwise_xor(me, j), 1 if GATHER == "zl" else 0, keepdims=False
    ).reshape(n_slab, width)
    ops = lax.dynamic_index_in_dim(sphere_ops.reshape(nc, n_ops, width), core, 0, keepdims=False)
    near = jnp.concatenate([pick(1), ops, pick(3)], axis=0)
    own = jnp.concatenate([pick(0), ops], axis=0)
    to_far = pick(2)
    got_near = swap(near, GATHER, 1)
    far = jnp.concatenate([to_far, ops, got_near[n_slab + n_ops :], got_near[n_slab : n_slab + n_ops]], axis=0)
    got_far = swap(far, GATHER, 2)
    n_all = n_slab + n_ops
    stacked = jnp.stack([own, got_near[:n_all], got_far[:n_all], got_far[n_all:]])
    other = swap(stacked, "c", 1)
    both = [jnp.where(core == c, stacked, other) for c in range(nc)]
    got = jnp.stack(both, axis=1)
    odd, high = jnp.bitwise_and(me, 1) == 1, me >= 2
    pairs = [jnp.where(odd, got[j ^ 1], got[j]) for j in range(4)]
    got = jnp.stack([jnp.where(high, pairs[j ^ 2], pairs[j]) for j in range(4)])
    slab_g = got[:, :, :n_slab]
    ops_g = got[:, :, n_slab:].reshape(ng, nd, atoms, lm, lm)

    first_row = (lax.axis_index("x") * nzl + lax.axis_index("zl")) * own_rows
    own_orbitals = lax.dynamic_slice_in_dim(orbitals, first_row, own_rows, 0)
    own_factors = lax.dynamic_slice_in_dim(wave_terms, first_row, own_rows, 1)
    local = own_factors[:, :, None] * own_orbitals[None]

    mine = mine.sum(0)
    mine = gather(mine, THIRD).reshape((nzh, -1, sub, half))
    mine = mine.sum(0)
    coeffs = gather(mine, FOURTH).reshape(ny, ng, sub, half)
    coeffs = coeffs.transpose(1, 0, 2, 3).reshape(ng, atoms, lm, half)
    inner = jnp.einsum("gdalm,gamb->dgalb", ops_g, coeffs, precision=lax.Precision.HIGH)
    inner = inner.reshape(nd, ng, width, half)
    terms = jnp.einsum("gcws,dgsb->cdwb", slab_g, inner, precision=lax.Precision.HIGH)
    terms = terms.reshape(nc, nd, nr, own_rows, half).transpose(0, 2, 1, 3, 4)
    summed = exchange(terms.reshape(nc * nr, nd, own_rows, half), ("c", REDUCE))
    summed = summed.reshape(nc, nr, nd, own_rows, half).sum(1)
    summed = summed.transpose(1, 2, 0, 3).reshape(nd, own_rows, nb)
    return summed + local


def solution(mesh):
    fine = Mesh(mesh.devices.reshape(8, 3, 2, 4, 4), ("y", "zh", "c", "x", "zl"))
    wave, atom = ("y", "zh", "c"), ("x", "zl")
    return jax.shard_map(
        apply,
        mesh=fine,
        in_specs=(P(wave, atom), P(wave, None), P(None, atom, None, None), P(None, wave)),
        out_specs=P(None, wave + atom, None),
        check_vma=False,
    )
```

```python
import jax
import jax.numpy as jnp
from jax import lax
from jax.experimental import pallas as pl
from jax.experimental.pallas import tpu as pltpu
from jax.sharding import Mesh, PartitionSpec as P


GATHER, REDUCE = "zl", "x"
THIRD, FOURTH = ("zh",), ("y", GATHER)
VMEM = pl.BlockSpec(memory_space=pltpu.VMEM)


def exchange(blocks, axes):
    return lax.all_to_all(blocks, axes, 0, 0, tiled=True)


def gather(block, axes):
    n = lax.axis_size(axes)
    return exchange(jnp.broadcast_to(block[None], (n,) + block.shape), axes)


def swap(block, axis, bit):
    n = lax.axis_size(axis)
    return lax.ppermute(block, axis, [(i, i ^ bit) for i in range(n)])


def split(a):
    high = a.astype(jnp.bfloat16)
    return high, (a - high.astype(jnp.float32)).astype(jnp.bfloat16)


def dot3(a, b, dims=(((1,), (0,)), ((), ()))):
    (ah, al), (bh, bl) = a, b
    f = lambda u, v: lax.dot_general(u, v, dims, preferred_element_type=jnp.float32)
    return f(ah, bh) + (f(ah, bl) + f(al, bh))


def first_kernel(slab_ref, orb_ref, out_ref):
    n, sub, half = out_ref.shape
    nc = orb_ref.shape[1] // half
    part = dot3(split(slab_ref[...].T), split(orb_ref[...]))
    for y in range(n // nc):
        for c in range(nc):
            out_ref[y * nc + c] = part[y * sub : (y + 1) * sub, c * half : (c + 1) * half]


def apply(slab, orbitals, sphere_ops, wave_terms):
    ny, nzh, nc, nx, nzl = (lax.axis_size(n) for n in ("y", "zh", "c", "x", "zl"))
    ng, nr = lax.axis_size(GATHER), lax.axis_size(REDUCE)
    rows, width = slab.shape
    nb = orbitals.shape[1]
    half = nb // nc
    own_rows = rows // (nx * nzl)
    nd, atoms, lm = sphere_ops.shape[:3]
    sub = width // ny
    me, core = lax.axis_index(GATHER), lax.axis_index("c")
    f32 = lambda *s: jax.ShapeDtypeStruct(s, jnp.float32)

    part = pl.pallas_call(
        first_kernel, out_shape=f32(ny * nc, sub, half), in_specs=[VMEM] * 2, out_specs=VMEM, name="first_dot"
    )(slab, orbitals)
    mine = exchange(part, ("y", "c"))

    n_slab, n_ops = nr * own_rows, nd * lm // nc
    rowset = slab.reshape(nx, nzl, own_rows, width)
    pick = lambda j: lax.dynamic_index_in_dim(
        rowset, jnp.bitwise_xor(me, j), 1 if GATHER == "zl" else 0, keepdims=False
    ).reshape(n_slab, width)
    ops = lax.dynamic_index_in_dim(sphere_ops.reshape(nc, n_ops, width), core, 0, keepdims=False)
    sent_a = jnp.concatenate([pick(2), ops, pick(3)], axis=0)
    own = jnp.concatenate([pick(0), ops], axis=0)
    beside = pick(1)
    got_a = swap(sent_a, GATHER, 2)
    sent_b = jnp.concatenate([beside, ops, got_a[n_slab + n_ops :], got_a[n_slab : n_slab + n_ops]], axis=0)
    got_b = swap(sent_b, GATHER, 1)
    n_all = n_slab + n_ops
    stacked = jnp.stack([own, got_b[:n_all], got_a[:n_all], got_b[n_all:]])
    other = swap(stacked, "c", 1)
    both = [jnp.where(core == c, stacked, other) for c in range(nc)]
    got = jnp.stack(both, axis=1)
    odd, high = jnp.bitwise_and(me, 1) == 1, me >= 2
    pairs = [jnp.where(odd, got[j ^ 1], got[j]) for j in range(4)]
    got = jnp.stack([jnp.where(high, pairs[j ^ 2], pairs[j]) for j in range(4)])
    slab_g = got[:, :, :n_slab]
    ops_g = got[:, :, n_slab:].reshape(ng, nd, atoms, lm, lm)

    first_row = (lax.axis_index("x") * nzl + lax.axis_index("zl")) * own_rows
    own_orbitals = lax.dynamic_slice_in_dim(orbitals, first_row, own_rows, 0)
    own_factors = lax.dynamic_slice_in_dim(wave_terms, first_row, own_rows, 1)
    local = own_factors[:, :, None] * own_orbitals[None]

    mine = mine.sum(0)
    mine = gather(mine, THIRD).reshape((nzh, -1, sub, half))
    mine = mine.sum(0)
    coeffs = gather(mine, FOURTH).reshape(ny, ng, sub, half)
    coeffs = coeffs.transpose(1, 0, 2, 3).reshape(ng, atoms, lm, half)
    inner = jnp.einsum("gdalm,gamb->dgalb", ops_g, coeffs, precision=lax.Precision.HIGH)
    inner = inner.reshape(nd, ng, width, half)
    terms = jnp.einsum("gcws,dgsb->cdwb", slab_g, inner, precision=lax.Precision.HIGH)
    terms = terms.reshape(nc, nd, nr, own_rows, half).transpose(0, 2, 1, 3, 4)
    summed = exchange(terms.reshape(nc * nr, nd, own_rows, half), ("c", REDUCE))
    summed = summed.reshape(nc, nr, nd, own_rows, half).sum(1)
    summed = summed.transpose(1, 2, 0, 3).reshape(nd, own_rows, nb)
    return summed + local


def solution(mesh):
    fine = Mesh(mesh.devices.reshape(8, 3, 2, 4, 4), ("y", "zh", "c", "x", "zl"))
    wave, atom = ("y", "zh", "c"), ("x", "zl")
    return jax.shard_map(
        apply,
        mesh=fine,
        in_specs=(P(wave, atom), P(wave, None), P(None, atom, None, None), P(None, wave)),
        out_specs=P(None, wave + atom, None),
        check_vma=False,
    )
```

```python
import jax
import jax.numpy as jnp
from jax import lax
from jax.experimental import pallas as pl
from jax.experimental.pallas import tpu as pltpu
from jax.sharding import Mesh, PartitionSpec as P


GATHER, REDUCE = "zm", ("x", "zk")
FOURTH = (GATHER, "y")
VMEM = pl.BlockSpec(memory_space=pltpu.VMEM)


def exchange(blocks, axes):
    return lax.all_to_all(blocks, axes, 0, 0, tiled=True)


def gather(block, axes):
    n = lax.axis_size(axes)
    return exchange(jnp.broadcast_to(block[None], (n,) + block.shape), axes)


def swap(block, axis, bit):
    n = lax.axis_size(axis)
    return lax.ppermute(block, axis, [(i, i ^ bit) for i in range(n)])


def split(a):
    high = a.astype(jnp.bfloat16)
    return high, (a - high.astype(jnp.float32)).astype(jnp.bfloat16)


def dot3(a, b, dims=(((1,), (0,)), ((), ()))):
    (ah, al), (bh, bl) = a, b
    f = lambda u, v: lax.dot_general(u, v, dims, preferred_element_type=jnp.float32)
    return f(ah, bh) + (f(ah, bl) + f(al, bh))


def first_kernel(slab_ref, orb_ref, out_ref):
    n, sub, half = out_ref.shape
    nc = orb_ref.shape[1] // half
    part = dot3(split(slab_ref[...].T), split(orb_ref[...]))
    for y in range(n // nc):
        for c in range(nc):
            out_ref[c * (n // nc) + y] = part[y * sub : (y + 1) * sub, c * half : (c + 1) * half]


def apply(slab, orbitals, sphere_ops, wave_terms):
    ny, _, nc, nx, nzk = (lax.axis_size(n) for n in ("y", "zh", "c", "x", "zk"))
    ng, nr = lax.axis_size(GATHER), nx * nzk
    rows, width = slab.shape
    nb = orbitals.shape[1]
    half = nb // nc
    own_rows = rows // (ng * nr)
    nd, atoms, lm = sphere_ops.shape[:3]
    sub = width // ny
    me, core = lax.axis_index(GATHER), lax.axis_index("c")
    f32 = lambda *s: jax.ShapeDtypeStruct(s, jnp.float32)

    part = pl.pallas_call(
        first_kernel, out_shape=f32(ny * nc, sub, half), in_specs=[VMEM] * 2, out_specs=VMEM, name="first_dot"
    )(slab, orbitals)
    mine = exchange(part, ("c", "y"))

    n_slab, n_ops = nr * own_rows, nd * lm // nc
    rowset = slab.reshape(nx, ng, nzk, own_rows, width)
    pick = lambda g: lax.dynamic_index_in_dim(rowset, g, 1, keepdims=False).reshape(n_slab, width)
    ops = lax.dynamic_index_in_dim(sphere_ops.reshape(nc, n_ops, width), core, 0, keepdims=False)
    sent = jnp.concatenate([pick(1 - me), ops], axis=0)
    own = jnp.concatenate([pick(me), ops], axis=0)
    moved = swap(sent, GATHER, 1)
    stacked = jnp.stack([own, moved])
    other = swap(stacked, "c", 1)
    both = [jnp.where(core == c, stacked, other) for c in range(nc)]
    got = jnp.stack(both, axis=1)
    got = jnp.stack([jnp.where(me == 0, got[0], got[1]), jnp.where(me == 0, got[1], got[0])])
    slab_g = got[:, :, :n_slab]
    ops_g = got[:, :, n_slab:].reshape(ng, nd, atoms, lm, lm)

    first_row = lax.axis_index(("x", "zm", "zk")) * own_rows
    own_orbitals = lax.dynamic_slice_in_dim(orbitals, first_row, own_rows, 0)
    own_factors = lax.dynamic_slice_in_dim(wave_terms, first_row, own_rows, 1)
    local = own_factors[:, :, None] * own_orbitals[None]

    mine = mine.sum(0)
    mine = lax.psum(mine, "zh")
    coeffs = gather(mine, FOURTH).reshape(ng, ny, sub, half)
    coeffs = coeffs.reshape(ng, atoms, lm, half)
    inner = jnp.einsum("gdalm,gamb->dgalb", ops_g, coeffs, precision=lax.Precision.HIGH)
    inner = inner.reshape(nd, ng, width, half)
    terms = jnp.einsum("gcws,dgsb->cdwb", slab_g, inner, precision=lax.Precision.HIGH)
    terms = terms.reshape(nc, nd, nr, own_rows, half).transpose(0, 2, 1, 3, 4)
    summed = exchange(terms.reshape(nc * nr, nd, own_rows, half), ("c",) + REDUCE)
    summed = summed.reshape(nc, nr, nd, own_rows, half).sum(1)
    summed = summed.transpose(1, 2, 0, 3).reshape(nd, own_rows, nb)
    return summed + local


def solution(mesh):
    fine = Mesh(mesh.devices.reshape(8, 3, 2, 4, 2, 2), ("y", "zh", "c", "x", "zm", "zk"))
    wave, atom = ("y", "zh", "c"), ("x", "zm", "zk")
    return jax.shard_map(
        apply,
        mesh=fine,
        in_specs=(P(wave, atom), P(wave, None), P(None, atom, None, None), P(None, wave)),
        out_specs=P(None, wave + atom, None),
        check_vma=False,
    )
```

```python
import jax
import jax.numpy as jnp
from jax import lax
from jax.experimental import pallas as pl
from jax.experimental.pallas import tpu as pltpu
from jax.sharding import Mesh, PartitionSpec as P


GATHER, REDUCE = "zl", "x"
THIRD, FOURTH = ("zh",), (GATHER, "y")
VMEM = pl.BlockSpec(memory_space=pltpu.VMEM)


def exchange(blocks, axes):
    return lax.all_to_all(blocks, axes, 0, 0, tiled=True)


def gather(block, axes):
    n = lax.axis_size(axes)
    return exchange(jnp.broadcast_to(block[None], (n,) + block.shape), axes)


def swap(block, axis, bit):
    n = lax.axis_size(axis)
    return lax.ppermute(block, axis, [(i, i ^ bit) for i in range(n)])


def split(a):
    high = a.astype(jnp.bfloat16)
    return high, (a - high.astype(jnp.float32)).astype(jnp.bfloat16)


def dot3(a, b, dims=(((1,), (0,)), ((), ()))):
    (ah, al), (bh, bl) = a, b
    f = lambda u, v: lax.dot_general(u, v, dims, preferred_element_type=jnp.float32)
    return f(ah, bh) + (f(ah, bl) + f(al, bh))


def first_kernel(slab_ref, orb_ref, out_ref):
    n, sub, half = out_ref.shape
    nc = orb_ref.shape[1] // half
    part = dot3(split(slab_ref[...]), split(orb_ref[...]), (((0,), (0,)), ((), ())))
    for y in range(n // nc):
        for c in range(nc):
            out_ref[c * (n // nc) + y] = part[y * sub : (y + 1) * sub, c * half : (c + 1) * half]


def apply(slab, orbitals, sphere_ops, wave_terms):
    ny, nzh, nc, nx, nzl = (lax.axis_size(n) for n in ("y", "zh", "c", "x", "zl"))
    ng, nr = lax.axis_size(GATHER), lax.axis_size(REDUCE)
    rows, width = slab.shape
    nb = orbitals.shape[1]
    half = nb // nc
    own_rows = rows // (nx * nzl)
    nd, atoms, lm = sphere_ops.shape[:3]
    sub = width // ny
    me, core = lax.axis_index(GATHER), lax.axis_index("c")
    f32 = lambda *s: jax.ShapeDtypeStruct(s, jnp.float32)

    part = pl.pallas_call(
        first_kernel, out_shape=f32(ny * nc, sub, half), in_specs=[VMEM] * 2, out_specs=VMEM, name="first_dot"
    )(slab, orbitals)
    mine = exchange(part, ("c", "y"))

    n_slab, n_ops = nr * own_rows, nd * lm // nc
    rowset = slab.reshape(nx, nzl, own_rows, width)
    pick = lambda j: lax.dynamic_index_in_dim(
        rowset, jnp.bitwise_xor(me, j), 1 if GATHER == "zl" else 0, keepdims=False
    ).reshape(n_slab, width)
    ops = lax.dynamic_index_in_dim(sphere_ops.reshape(nc, n_ops, width), core, 0, keepdims=False)
    sent_a = jnp.concatenate([pick(2), ops, pick(3)], axis=0)
    own = jnp.concatenate([pick(0), ops], axis=0)
    beside = pick(1)
    got_a = swap(sent_a, GATHER, 2)
    sent_b = jnp.concatenate([beside, ops, got_a[n_slab + n_ops :], got_a[n_slab : n_slab + n_ops]], axis=0)
    got_b = swap(sent_b, GATHER, 1)
    n_all = n_slab + n_ops
    stacked = jnp.stack([own, got_b[:n_all], got_a[:n_all], got_b[n_all:]])
    other = swap(stacked, "c", 1)
    both = [jnp.where(core == c, stacked, other) for c in range(nc)]
    got = jnp.stack(both, axis=1)
    odd, high = jnp.bitwise_and(me, 1) == 1, me >= 2
    pairs = [jnp.where(odd, got[j ^ 1], got[j]) for j in range(4)]
    got = jnp.stack([jnp.where(high, pairs[j ^ 2], pairs[j]) for j in range(4)])
    slab_g = got[:, :, :n_slab]
    ops_g = got[:, :, n_slab:].reshape(ng, nd, atoms, lm, lm)

    first_row = (lax.axis_index("x") * nzl + lax.axis_index("zl")) * own_rows
    own_orbitals = lax.dynamic_slice_in_dim(orbitals, first_row, own_rows, 0)
    own_factors = lax.dynamic_slice_in_dim(wave_terms, first_row, own_rows, 1)
    local = own_factors[:, :, None] * own_orbitals[None]

    mine = mine.sum(0)
    mine = gather(mine, THIRD).reshape((nzh, -1, sub, half))
    mine = mine.sum(0)
    coeffs = gather(mine, FOURTH).reshape(ng, ny, sub, half)
    coeffs = coeffs.reshape(ng, atoms, lm, half)
    inner = jnp.einsum("gdalm,gamb->dgalb", ops_g, coeffs, precision=lax.Precision.HIGH)
    inner = inner.reshape(nd, ng, width, half)
    terms = jnp.einsum("gcws,dgsb->cdwb", slab_g, inner, precision=lax.Precision.HIGH)
    terms = terms.reshape(nc, nd, nr, own_rows, half).transpose(0, 2, 1, 3, 4)
    summed = exchange(terms.reshape(nc * nr, nd, own_rows, half), ("c", REDUCE))
    summed = summed.reshape(nc, nr, nd, own_rows, half).sum(1)
    summed = summed.transpose(1, 2, 0, 3).reshape(nd, own_rows, nb)
    return summed + local


def solution(mesh):
    fine = Mesh(mesh.devices.reshape(8, 3, 2, 4, 4), ("y", "zh", "c", "x", "zl"))
    wave, atom = ("y", "zh", "c"), ("x", "zl")
    return jax.shard_map(
        apply,
        mesh=fine,
        in_specs=(P(wave, atom), P(wave, None), P(None, atom, None, None), P(None, wave)),
        out_specs=P(None, wave + atom, None),
        check_vma=False,
    )
```
